32 devices in a mesh: sec: 4 (over y, x), strip: 8 (over z, core).
Axes of the slice: x: 2, y: 2, z: 4, core: 2. Of those that a mesh axis runs over, the one named last changes fastest.
Arguments:
- features: bfloat16 [4, 96, 128, 128], P('sec', 'strip'), may hold values from -6 to 6
- offsets: int32 [4], replicated, may hold values from -2 to 2
- state: float32 [2, 4, 96, 128], P(None, 'sec', 'strip'), may hold values from -6 to 6
- w_first: bfloat16 [3, 3, 162, 128], replicated, may hold values from -0.15625 to 0.15625
- b_first: float32 [128], replicated, may hold values from -3 to 3
- w_second: bfloat16 [3, 3, 128, 128], replicated, may hold values from -0.1875 to 0.1875
- b_second: float32 [128], replicated, may hold values from -3 to 3
- w_third: bfloat16 [3, 3, 128, 2], replicated, may hold values from -0.1875 to 0.1875
Outputs:
- updated: float32 [2, 4, 96, 128], P(None, 'sec', 'strip')
The draws below stay inside these ranges and needn't reach their ends.
Inputs may be any that keep to these rules, and one draw needn't show every extreme that they name: offsets[s] is the integer row offset of section s+1 against section s; the last entry is not used.
All inputs are finite; a program needn't handle non-finite values.
Results may differ from the reference program's by a relative error of at most 0.0029.
Values may be sent and summed in bfloat16 or wider, within the bound.
A program may use at most 64 MiB of HBM per device.

```python
import jax
import jax.numpy as jnp
from jax import lax

C = 128
HID = 128
COLS = 128
SECTIONS = 4
ROWS = 96


def plant(result, key, low, high):
    spot = [jax.random.randint(jax.random.fold_in(key, axis), (), 0, length) for axis, length in enumerate(result.shape)]
    main_axis = result.shape.index(max(result.shape))
    beside = spot[:main_axis] + [(spot[main_axis] + 1) % result.shape[main_axis]] + spot[main_axis + 1:]
    return result.at[tuple(spot)].set(low).at[tuple(beside)].set(high)


def block_levels(key, dims, shards, least, top_value):
    def one(axis_at, blocks):
        heights = jax.random.uniform(jax.random.fold_in(jax.random.fold_in(key, 6), axis_at), (blocks,), jnp.float32, least / len(shards), top_value / len(shards))
        return jnp.repeat(jnp.exp(heights), dims[axis_at] // blocks).reshape((-1,) + (1,) * (len(dims) - axis_at - 1))

    loudness = one(*shards[0])
    for cut in shards[1:]:
        loudness = loudness * one(*cut)
    return loudness


def bell_draw(stream_key, shape, spread, most, split=(), held_as=jnp.bfloat16):
    drawn = spread * jax.random.normal(stream_key, shape, jnp.float32)
    if split:
        drawn = drawn * block_levels(stream_key, shape, split, -0.22, 0.18)
    return jnp.clip(drawn, -most, most).astype(held_as)


def setup_inputs(seed: int = 0) -> dict:
    seeds = jax.random.split(jax.random.key(seed), 9)
    features = bell_draw(seeds[0], (SECTIONS, ROWS, COLS, C), 1.0, 6.0, ((0, 4), (1, 8)))
    offsets = plant(jax.random.randint(seeds[1], (SECTIONS,), -2, 3), jax.random.fold_in(seeds[1], 1), -2, 2).astype(jnp.int32)
    state = bell_draw(seeds[2], (2, SECTIONS, ROWS, COLS), 1.0, 6.0, ((1, 4), (2, 8)), jnp.float32)
    w_first = bell_draw(seeds[3], (3, 3, 162, HID), (9 * 162) ** -0.5, 0.15625)
    b_first = bell_draw(seeds[4], (HID,), 0.5, 3.0, (), jnp.float32)
    w_second = bell_draw(seeds[5], (3, 3, HID, HID), (9 * HID) ** -0.5, 0.1875)
    b_second = bell_draw(seeds[6], (HID,), 0.5, 3.0, (), jnp.float32)
    w_third = bell_draw(seeds[7], (3, 3, HID, 2), (9 * HID) ** -0.5, 0.1875)
    return {"features": features, "offsets": offsets, "state": state, "w_first": w_first, "b_first": b_first, "w_second": w_second, "b_second": b_second, "w_third": w_third}


def corr_pair(mine, other, shift):
    padded = jnp.pad(other.astype(jnp.float32), ((6, 6), (4, 4), (0, 0)))
    mine_f = mine.astype(jnp.float32)
    planes = []
    for row_step in range(-4, 5):
        start = (6 + row_step + shift).astype(jnp.int32)
        taken = lax.dynamic_slice_in_dim(padded, start, ROWS, 0)
        for col_step in range(-4, 5):
            planes.append(jnp.sum(mine_f * taken[:, 4 + col_step:4 + col_step + COLS], axis=-1))
    return jnp.stack(planes)


def convolve(values, kernel, layout):
    return lax.conv_general_dilated(values[None], kernel, (1, 1), ((1, 1), (1, 1)),
                                    dimension_numbers=(layout, "HWIO", "NHWC"),
                                    preferred_element_type=jnp.float32)[0]


def reference(features, offsets, state, w_first, b_first, w_second, b_second, w_third):
    empty = jnp.zeros_like(features[:1])
    below_all = jnp.concatenate([empty, features[:-1]], 0)
    above_all = jnp.concatenate([features[1:], empty], 0)
    shift_above = offsets.astype(jnp.int32)
    shift_below = jnp.concatenate([jnp.zeros((1,), jnp.int32), -offsets[:-1].astype(jnp.int32)], 0)

    def one_section(items):
        mine, below, above, down_shift, up_shift = items
        corr = jnp.concatenate([corr_pair(mine, below, down_shift), corr_pair(mine, above, up_shift)], 0)
        corr = (corr * (C ** -0.5)).astype(jnp.bfloat16)
        hidden_one = jax.nn.relu(convolve(corr, w_first, "NCHW") + b_first).astype(jnp.bfloat16)
        hidden_two = jax.nn.relu(convolve(hidden_one, w_second, "NHWC") + b_second).astype(jnp.bfloat16)
        delta = convolve(hidden_two, w_third, "NHWC")
        return jnp.moveaxis(delta, 2, 0)

    deltas = lax.map(one_section, (features, below_all, above_all, shift_below, shift_above))
    return state + jnp.moveaxis(deltas, 1, 0)
```

```python
import functools

import jax
import jax.numpy as jnp
from jax import lax
from jax.experimental import pallas as pl
from jax.experimental.pallas import tpu as pltpu
from jax.sharding import PartitionSpec as P

SIDE = 9
STEP = 3
TAPS = 9
VMEM = pl.BlockSpec(memory_space=pltpu.VMEM)
SMEM = pl.BlockSpec(memory_space=pltpu.SMEM)


def group_of(rows):
    return max(g for g in range(1, 8) if rows % g == 0)


def exchange(secs, strips, feat, mine, wide, send_sem, recv_sem):
    rows = feat.shape[1]
    count = rows // STEP
    sec, strip = lax.axis_index("sec"), lax.axis_index("strip")
    odd = lax.rem(sec, 2)
    partner = sec + 1 - 2 * odd
    near, far = 1 - odd, odd
    relay_to, relay_from = sec + 2 - 4 * odd, sec - 2 + 4 * odd
    has_to = (relay_to >= 0) & (relay_to < secs)
    has_from = (relay_from >= 0) & (relay_from < secs)
    has_low, has_high = strip > 0, strip < strips - 1

    barrier = pltpu.get_barrier_semaphore()
    greeted = (
        (None, partner, strip),
        (has_to, relay_to, strip),
        (has_from, relay_from, strip),
        (has_low, sec, strip - 1),
        (has_high, sec, strip + 1),
    )

    def when(cond, act):
        if cond is None:
            act()
        else:
            pl.when(cond)(act)

    for cond, a, b in greeted:
        when(cond, lambda a=a, b=b: pl.semaphore_signal(barrier, inc=1, device_id=(a, b), device_id_type=pl.DeviceIdType.MESH))

    zero = jnp.zeros((SIDE,) + wide.shape[2:], wide.dtype)

    @pl.when(jnp.logical_not(has_from))
    def _():
        wide[far] = jnp.zeros(wide.shape[1:], wide.dtype)

    @pl.when(jnp.logical_not(has_low))
    def _():
        wide[near, 0:SIDE] = zero
        wide[far, 0:SIDE] = zero
        mine[0:STEP] = zero[:STEP]

    @pl.when(jnp.logical_not(has_high))
    def _():
        wide[near, SIDE + rows:] = zero
        wide[far, SIDE + rows:] = zero
        mine[STEP + rows:] = zero[:STEP]

    mine[STEP:STEP + rows] = feat[0]

    pl.semaphore_wait(barrier, 1 + sum(cond.astype(jnp.int32) for cond, _, _ in greeted[1:]))

    waits = []
    number = [0]

    def copy(src, dst, a, b, sends, gets):
        at = number[0]
        number[0] += 1
        made = pltpu.make_async_remote_copy(
            src_ref=src, dst_ref=dst, send_sem=send_sem.at[at], recv_sem=recv_sem.at[at],
            device_id=(a, b), device_id_type=pl.DeviceIdType.MESH,
        )
        when(sends, made.start)
        waits.append((sends, made.wait_send))
        return lambda: when(gets, made.wait_recv)

    def both(x, y):
        return y if x is None else x & y

    def down(slot, q, known):
        return copy(
            wide.at[slot, pl.ds(SIDE + STEP * q, STEP)], wide.at[slot, pl.ds(SIDE + rows + STEP * q, STEP)],
            sec, strip - 1, both(known, has_low), both(known, has_high),
        )

    def up(slot, q, known):
        return copy(
            wide.at[slot, pl.ds(SIDE + STEP * q, STEP)], wide.at[slot, pl.ds(SIDE + STEP * q - rows, STEP)],
            sec, strip + 1, both(known, has_high), both(known, has_low),
        )

    order = list(range(count))
    direct = [
        copy(feat.at[0, pl.ds(STEP * q, STEP)], wide.at[far, pl.ds(SIDE + STEP * q, STEP)], partner, strip, None, None)
        for q in order
    ]
    last = []
    last.append(copy(feat.at[0, pl.ds(0, STEP)], mine.at[pl.ds(STEP + rows, STEP)], sec, strip - 1, has_low, has_high))
    last.append(copy(feat.at[0, pl.ds(rows - STEP, STEP)], mine.at[pl.ds(0, STEP)], sec, strip + 1, has_high, has_low))

    def sides(slot, q, known):
        if STEP * q < SIDE:
            last.append(down(slot, q, known))
        if STEP * q >= rows - SIDE:
            last.append(up(slot, q, known))

    relayed = []
    for q in order + [count]:
        if q < count:
            direct[q]()
            relayed.append(copy(
                wide.at[near, pl.ds(SIDE + STEP * q, STEP)], wide.at[far, pl.ds(SIDE + STEP * q, STEP)],
                relay_to, strip, has_to, has_from,
            ))
            sides(near, q, None)
        if q >= 1:
            relayed[q - 1]()
            sides(far, q - 1, has_from)
    for wait in last:
        wait()
    for cond, wait in waits:
        when(cond, wait)


def convolve(source, weight, bias, target):
    rows, cols, width = target.shape
    depth = source.shape[2]
    group = group_of(rows)
    at_col = lax.broadcasted_iota(jnp.int32, (cols, width), 0)

    def step(g, carry):
        base = g * group
        taken = jnp.concatenate(
            [source[pl.ds(base + d, group)].reshape(group * cols, depth) for d in range(3)], axis=1
        )
        sums = jnp.dot(taken, weight[...], preferred_element_type=jnp.float32)
        for i in range(group):
            one = sums[i * cols:(i + 1) * cols]
            before = jnp.where(at_col == 0, 0.0, pltpu.roll(one[:, :width], 1, 0))
            after = jnp.where(at_col == cols - 1, 0.0, pltpu.roll(one[:, 2 * width:], cols - 1, 0))
            total = one[:, width:2 * width] + before + after + bias[...]
            target[base + i] = jnp.maximum(total, 0.0).astype(target.dtype)
        return carry

    lax.fori_loop(0, rows // group, step, 0)


def skewed(block, shift):
    rows, cols = block.shape
    pieces = []
    start = 0
    for top in range(0, rows, 8):
        if (shift + top) % cols + 7 > cols:
            if top > start:
                pieces.append(pltpu.roll(block[start:top], (shift + start) % cols, 1, stride=1, stride_axis=0))
            crossing = pltpu.roll(block[top:top + 8], (shift + top - 8) % cols, 1, stride=1, stride_axis=0)
            pieces.append(pltpu.roll(crossing, 8, 1))
            start = top + 8
    if start < rows:
        pieces.append(pltpu.roll(block[start:], (shift + start) % cols, 1, stride=1, stride_axis=0))
    return jnp.concatenate(pieces, axis=0)


def kernel(secs, strips, feat, offsets, w_one, b_one, w_two, b_two, w_three, out,
           mine, wide, corr, hid_one, hid_two, wide_one, wide_two, send_sem, recv_sem):
    rows, cols, chans = feat.shape[1:]
    hid = b_one.shape[1]
    planes = w_one.shape[2]
    depth = corr.shape[2]
    sec, strip = lax.axis_index("sec"), lax.axis_index("strip")

    for d in range(3):
        for e in range(3):
            if planes < depth:
                wide_one[d * depth:(d + 1) * depth, (2 - e) * hid:(3 - e) * hid] = jnp.zeros((depth, hid), wide_one.dtype)
            wide_one[d * depth:d * depth + planes, (2 - e) * hid:(3 - e) * hid] = w_one[d, e]
            wide_two[d * hid:(d + 1) * hid, (2 - e) * hid:(3 - e) * hid] = w_two[d, e]

    exchange(secs, strips, feat, mine, wide, send_sem, recv_sem)

    shifts = (
        jnp.where(sec > 0, -offsets[jnp.maximum(sec - 1, 0)], 0),
        jnp.where(sec < secs - 1, offsets[sec], 0),
    )
    scale = chans ** (-0.5)
    lane = lax.broadcasted_iota(jnp.int32, (cols, cols), 1)
    col = lax.broadcasted_iota(jnp.int32, (cols, cols), 0)
    flip = (lane + col == cols - 1).astype(mine.dtype)
    gains = []
    for tile in range(depth // cols):
        plane = lane + tile * cols
        other = cols - 1 - col + lax.rem(plane, TAPS) - 4
        gains.append(jnp.where((other >= 0) & (other < cols) & (plane < planes), scale, 0.0))

    def correlate(r, carry):
        here = jnp.dot(flip, mine[r], preferred_element_type=jnp.float32).astype(mine.dtype)
        found = [jnp.zeros((cols, cols), jnp.float32) for _ in gains]
        for j in range(2):
            there = wide[j, pl.ds(r + 2 + shifts[j], TAPS)].reshape(TAPS * cols, chans)
            products = lax.dot_general(here, there, (((1,), (1,)), ((), ())), preferred_element_type=jnp.float32)
            for a in range(TAPS):
                first = (j * TAPS + a) * TAPS
                turned = skewed(products[:, a * cols:(a + 1) * cols], first + 5)
                for tile in range(len(gains)):
                    low = first - tile * cols
                    if low < cols and low + TAPS > 0:
                        found[tile] = jnp.where((lane >= low) & (lane < low + TAPS), turned, found[tile])
        for tile, gain in enumerate(gains):
            corr[r, :, tile * cols:(tile + 1) * cols] = (found[tile] * gain).astype(corr.dtype)
        return carry

    lax.fori_loop(0, rows + 6, correlate, 0)

    convolve(corr, wide_one, b_one, hid_one)

    @pl.when(strip == 0)
    def _():
        hid_one[0:2] = jnp.zeros((2, cols, hid), hid_one.dtype)

    @pl.when(strip == strips - 1)
    def _():
        hid_one[rows + 2:] = jnp.zeros((2, cols, hid), hid_one.dtype)

    convolve(hid_one, wide_two, b_two, hid_two)

    @pl.when(strip == 0)
    def _():
        hid_two[0:1] = jnp.zeros((1, cols, hid), hid_two.dtype)

    @pl.when(strip == strips - 1)
    def _():
        hid_two[rows + 1:] = jnp.zeros((1, cols, hid), hid_two.dtype)

    taps = lax.dot_general(
        w_three[...], hid_two[...].reshape((rows + 2) * cols, hid), (((1,), (1,)), ((), ())),
        preferred_element_type=jnp.float32,
    )
    at_lane = lax.broadcasted_iota(jnp.int32, (8, cols), 1)
    found = []
    for r in range(rows):
        total = sum(taps[8 * d:8 * d + 8, (r + d) * cols:(r + d + 1) * cols] for d in range(3))
        before = jnp.where(at_lane == 0, 0.0, pltpu.roll(total, 1, 1))
        after = jnp.where(at_lane == cols - 1, 0.0, pltpu.roll(total, cols - 1, 1))
        found.append(before[0:2] + total[2:4] + after[4:6])
    turned = jnp.dot(
        jnp.concatenate(found, axis=0), flip.astype(jnp.float32),
        preferred_element_type=jnp.float32, precision=lax.Precision.HIGHEST,
    )
    for r in range(rows):
        out[:, r, :] = turned[2 * r:2 * r + 2]


def body(secs, strips, features, offsets, state, w_first, b_first, w_second, b_second, w_third):
    _, rows, cols, chans = features.shape
    planes, hid = w_first.shape[2:]
    depth = -(-planes // cols) * cols
    parts = w_third.shape[3]
    thirds = jnp.pad(jnp.transpose(w_third[:, ::-1], (0, 1, 3, 2)).reshape(3, 3 * parts, hid), ((0, 0), (0, 8 - 3 * parts), (0, 0)))
    copies = 2 * (rows // STEP) + 4 * (SIDE // STEP) + 2
    bf16 = jnp.bfloat16
    delta = pl.pallas_call(
        functools.partial(kernel, secs, strips),
        out_shape=jax.ShapeDtypeStruct((parts, rows, cols), jnp.float32),
        in_specs=[VMEM, SMEM] + [VMEM] * 5,
        out_specs=VMEM,
        scratch_shapes=[
            pltpu.VMEM((rows + 6, cols, chans), bf16),
            pltpu.VMEM((2, rows + 2 * SIDE, cols, chans), bf16),
            pltpu.VMEM((rows + 6, cols, depth), bf16),
            pltpu.VMEM((rows + 4, cols, hid), bf16),
            pltpu.VMEM((rows + 2, cols, hid), bf16),
            pltpu.VMEM((3 * depth, 3 * hid), bf16),
            pltpu.VMEM((3 * hid, 3 * hid), bf16),
            pltpu.SemaphoreType.DMA((copies,)),
            pltpu.SemaphoreType.DMA((copies,)),
        ],
        compiler_params=pltpu.CompilerParams(collective_id=0, has_side_effects=True, vmem_limit_bytes=48 << 20),
    )(features, offsets, w_first, b_first.reshape(1, hid), w_second, b_second.reshape(1, hid), thirds.reshape(24, hid))
    return state + delta[:, None]


def solution(mesh):
    secs, strips = mesh.shape["sec"], mesh.shape["strip"]
    in_specs = (
        P("sec", "strip", None, None),
        P(),
        P(None, "sec", "strip", None),
        P(),
        P(),
        P(),
        P(),
        P(),
    )
    out_specs = P(None, "sec", "strip", None)
    return jax.shard_map(functools.partial(body, secs, strips), mesh=mesh, in_specs=in_specs, out_specs=out_specs, check_vma=False)
```

```python
import functools

import jax
import jax.numpy as jnp
from jax import lax
from jax.experimental import pallas as pl
from jax.experimental.pallas import tpu as pltpu
from jax.sharding import PartitionSpec as P

SIDE = 9
STEP = 3
TAPS = 9
VMEM = pl.BlockSpec(memory_space=pltpu.VMEM)
HBM = pl.BlockSpec(memory_space=pltpu.HBM)
SMEM = pl.BlockSpec(memory_space=pltpu.SMEM)


def group_of(rows):
    return max(g for g in range(1, 8) if rows % g == 0)


def exchange(secs, strips, feat, mine, near, far, send_sem, recv_sem, loads, prepare, turn, relate):
    rows = feat.shape[1]
    count = rows // STEP
    sec, strip = lax.axis_index("sec"), lax.axis_index("strip")
    odd = lax.rem(sec, 2)
    partner = sec + 1 - 2 * odd
    relay_to, relay_from = sec + 2 - 4 * odd, sec - 2 + 4 * odd
    has_to = (relay_to >= 0) & (relay_to < secs)
    has_from = (relay_from >= 0) & (relay_from < secs)
    has_low, has_high = strip > 0, strip < strips - 1

    barrier = pltpu.get_barrier_semaphore()
    greeted = (
        (None, partner, strip),
        (has_to, relay_to, strip),
        (has_from, relay_from, strip),
        (has_low, sec, strip - 1),
        (has_high, sec, strip + 1),
    )

    def when(cond, act):
        if cond is None:
            act()
        else:
            pl.when(cond)(act)

    for cond, a, b in greeted:
        when(cond, lambda a=a, b=b: pl.semaphore_signal(barrier, inc=1, device_id=(a, b), device_id_type=pl.DeviceIdType.MESH))

    for load in loads:
        load.start()
    pl.semaphore_wait(barrier, 1 + sum(cond.astype(jnp.int32) for cond, _, _ in greeted[1:]))

    waits = []
    number = [0]

    def copy(src, dst, a, b, sends, gets):
        at = number[0]
        number[0] += 1
        made = pltpu.make_async_remote_copy(
            src_ref=src, dst_ref=dst, send_sem=send_sem.at[at], recv_sem=recv_sem.at[at],
            device_id=(a, b), device_id_type=pl.DeviceIdType.MESH,
        )
        when(sends, made.start)
        waits.append((sends, made.wait_send))
        return lambda: when(gets, made.wait_recv)

    def both(x, y):
        return y if x is None else x & y

    def down(slot, q, known):
        return copy(
            slot.at[pl.ds(SIDE + STEP * q, STEP)], slot.at[pl.ds(SIDE + rows + STEP * q, STEP)],
            sec, strip - 1, both(known, has_low), both(known, has_high),
        )

    def up(slot, q, known):
        return copy(
            slot.at[pl.ds(SIDE + STEP * q, STEP)], slot.at[pl.ds(SIDE + STEP * q - rows, STEP)],
            sec, strip + 1, both(known, has_high), both(known, has_low),
        )

    order = list(range(count))
    direct = [
        copy(feat.at[0, pl.ds(STEP * q, STEP)], near.at[pl.ds(SIDE + STEP * q, STEP)], partner, strip, None, None)
        for q in order
    ]
    last = []
    last.append(copy(feat.at[0, pl.ds(0, STEP)], mine.at[pl.ds(STEP + rows, STEP)], sec, strip - 1, has_low, has_high))
    last.append(copy(feat.at[0, pl.ds(rows - STEP, STEP)], mine.at[pl.ds(0, STEP)], sec, strip + 1, has_high, has_low))

    zero = jnp.zeros((SIDE,) + near.shape[1:], near.dtype)

    @pl.when(jnp.logical_not(has_from))
    def _():
        far[...] = jnp.zeros(far.shape, far.dtype)

    @pl.when(jnp.logical_not(has_low))
    def _():
        near[0:SIDE] = zero
        far[0:SIDE] = zero
        mine[0:STEP] = zero[:STEP]

    @pl.when(jnp.logical_not(has_high))
    def _():
        near[SIDE + rows:] = zero
        far[SIDE + rows:] = zero
        mine[STEP + rows:] = zero[:STEP]

    prepare()
    for wait in last:
        wait()
    turn()
    relayed = []
    ends = ([], [])

    def sides(slot, q, known, found):
        if STEP * q < SIDE:
            found.append(down(slot, q, known))
        if STEP * q >= rows - SIDE:
            found.append(up(slot, q, known))

    for q in order + [count]:
        if q < count:
            direct[q]()
            relayed.append(copy(
                near.at[pl.ds(SIDE + STEP * q, STEP)], far.at[pl.ds(SIDE + STEP * q, STEP)],
                relay_to, strip, has_to, has_from,
            ))
            sides(near, q, None, ends[0])
        if q >= 1:
            relayed[q - 1]()
            sides(far, q - 1, has_from, ends[1])
    for wide, found, slot in zip((near, far), ends, (1 - odd, odd)):
        for wait in found:
            wait()
        relate(wide, slot)
    for cond, wait in waits:
        when(cond, wait)


def convolve(sources, weight, bias, target):
    rows, cols, width = target.shape
    depth = sources[0].shape[2]
    group = group_of(rows)
    at_col = lax.broadcasted_iota(jnp.int32, (cols, width), 0)

    def step(g, carry):
        base = g * group
        taken = jnp.concatenate(
            [s[pl.ds(base + d, group)].reshape(group * cols, depth) for d in range(3) for s in sources], axis=1
        )
        sums = jnp.dot(taken, weight[...], preferred_element_type=jnp.float32)
        for i in range(group):
            one = sums[i * cols:(i + 1) * cols]
            before = jnp.where(at_col == 0, 0.0, pltpu.roll(one[:, :width], 1, 0))
            after = jnp.where(at_col == cols - 1, 0.0, pltpu.roll(one[:, 2 * width:], cols - 1, 0))
            total = one[:, width:2 * width] + before + after + bias[...]
            target[base + i] = jnp.maximum(total, 0.0).astype(target.dtype)
        return carry

    lax.fori_loop(0, rows // group, step, 0)


def skewed(block, shift):
    rows, cols = block.shape
    pieces = []
    start = 0
    for top in range(0, rows, 8):
        if (shift + top) % cols + 7 > cols:
            if top > start:
                pieces.append(pltpu.roll(block[start:top], (shift + start) % cols, 1, stride=1, stride_axis=0))
            crossing = pltpu.roll(block[top:top + 8], (shift + top - 8) % cols, 1, stride=1, stride_axis=0)
            pieces.append(pltpu.roll(crossing, 8, 1))
            start = top + 8
    if start < rows:
        pieces.append(pltpu.roll(block[start:], (shift + start) % cols, 1, stride=1, stride_axis=0))
    return jnp.concatenate(pieces, axis=0)


def kernel(secs, strips, feat, offsets, w_one, b_one, w_two, b_two, w_three, out,
           mine, near, far, corr, hid_one, hid_two, held_one, held_two, wide_one, wide_two, thirds,
           send_sem, recv_sem, local_sem):
    rows, cols, chans = feat.shape[1:]
    hid = b_one.shape[1]
    planes = w_one.shape[2] // 2
    sec, strip = lax.axis_index("sec"), lax.axis_index("strip")
    loads = [
        pltpu.make_async_copy(feat.at[0], mine.at[pl.ds(STEP, rows)], local_sem.at[0]),
        pltpu.make_async_copy(w_one, held_one, local_sem.at[1]),
        pltpu.make_async_copy(w_two, held_two, local_sem.at[2]),
    ]

    def prepare():
        for d in range(3):
            thirds[8 * d:8 * d + 8] = jnp.zeros((8, hid), thirds.dtype)
            for e in range(3):
                thirds[8 * d + 4 - 2 * e:8 * d + 6 - 2 * e] = w_three[d, e].astype(thirds.dtype)
        for d in range(2 * 3):
            wide_one[d * cols + planes // 16 * 16:(d + 1) * cols] = jnp.zeros((cols - planes // 16 * 16, 3 * hid), wide_one.dtype)
        loads[1].wait()
        loads[2].wait()
        for d in range(3):
            for e in range(3):
                at = pl.ds((2 - e) * hid, hid)
                for j in range(2):
                    wide_one[pl.ds((2 * d + j) * cols, planes), at] = held_one[d, e, j * planes:(j + 1) * planes]
                wide_two[pl.ds(d * hid, hid), at] = held_two[d, e]
        loads[0].wait()

    scale = chans ** (-0.5)
    lane = lax.broadcasted_iota(jnp.int32, (cols, cols), 1)
    col = lax.broadcasted_iota(jnp.int32, (cols, cols), 0)
    flip = (lane + col == cols - 1).astype(mine.dtype)
    other = cols - 1 - col + lax.rem(lane, TAPS) - 4
    gain = jnp.where((other >= 0) & (other < cols) & (lane < planes), scale, 0.0)
    shifts = (
        jnp.where(sec > 0, -offsets[jnp.maximum(sec - 1, 0)], 0),
        jnp.where(sec < secs - 1, offsets[sec], 0),
    )

    def turn():
        def one(r, carry):
            mine[r] = jnp.dot(flip, mine[r], preferred_element_type=jnp.float32).astype(mine.dtype)
            return carry

        lax.fori_loop(0, rows + 6, one, 0)

    group = 6 if rows % 6 == 0 else 2

    def relate(wide, slot):
        shift = jnp.where(slot == 0, shifts[0], shifts[1])

        def step(g, carry):
            base = g * group
            here = mine[pl.ds(base, group)].reshape(group * cols, chans)
            products = {}
            for t in range(0, group + TAPS - 1, 2):
                low, high = max(0, t - TAPS + 1), min(group, t + 2)
                there = wide[pl.ds(base + 2 + shift + t, 2)].reshape(2 * cols, chans)
                tile = lax.dot_general(
                    here[low * cols:high * cols], there, (((1,), (1,)), ((), ())), preferred_element_type=jnp.float32
                )
                for i in range(low, high):
                    for u in range(2):
                        if 0 <= t + u - i < TAPS:
                            products[i, t + u - i] = tile[(i - low) * cols:(i - low + 1) * cols, u * cols:(u + 1) * cols]
            for i in range(group):
                found = skewed(products[i, 0], 5)
                for a in range(1, TAPS):
                    found = jnp.where(lane >= a * TAPS, skewed(products[i, a], a * TAPS + 5), found)
                corr[slot, base + i] = (found * gain).astype(corr.dtype)
            return carry

        lax.fori_loop(0, (rows + 6) // group, step, 0)

    exchange(secs, strips, feat, mine, near, far, send_sem, recv_sem, loads, prepare, turn, relate)

    convolve((corr.at[0], corr.at[1]), wide_one, b_one, hid_one)

    @pl.when(strip == 0)
    def _():
        hid_one[0:2] = jnp.zeros((2, cols, hid), hid_one.dtype)

    @pl.when(strip == strips - 1)
    def _():
        hid_one[rows + 2:] = jnp.zeros((2, cols, hid), hid_one.dtype)

    convolve((hid_one,), wide_two, b_two, hid_two)

    @pl.when(strip == 0)
    def _():
        hid_two[0:1] = jnp.zeros((1, cols, hid), hid_two.dtype)

    @pl.when(strip == strips - 1)
    def _():
        hid_two[rows + 1:] = jnp.zeros((1, cols, hid), hid_two.dtype)

    taps = lax.dot_general(
        thirds[...].astype(hid_two.dtype), hid_two[...].reshape((rows + 2) * cols, hid), (((1,), (1,)), ((), ())),
        preferred_element_type=jnp.float32,
    )
    at_lane = lax.broadcasted_iota(jnp.int32, (8, cols), 1)
    found = []
    for r in range(rows):
        total = sum(taps[8 * d:8 * d + 8, (r + d) * cols:(r + d + 1) * cols] for d in range(3))
        before = jnp.where(at_lane == 0, 0.0, pltpu.roll(total, 1, 1))
        after = jnp.where(at_lane == cols - 1, 0.0, pltpu.roll(total, cols - 1, 1))
        found.append(before[0:2] + total[2:4] + after[4:6])
    turned = jnp.dot(
        jnp.concatenate(found, axis=0), flip.astype(jnp.float32),
        preferred_element_type=jnp.float32, precision=lax.Precision.HIGHEST,
    )
    for r in range(rows):
        out[:, r, :] = turned[2 * r:2 * r + 2]


def body(secs, strips, features, offsets, state, w_first, b_first, w_second, b_second, w_third):
    _, rows, cols, chans = features.shape
    hid = w_first.shape[3]
    parts = w_third.shape[3]
    copies = 2 * (rows // STEP) + 4 * (SIDE // STEP) + 2
    bf16 = jnp.bfloat16
    delta = pl.pallas_call(
        functools.partial(kernel, secs, strips),
        out_shape=jax.ShapeDtypeStruct((parts, rows, cols), jnp.float32),
        in_specs=[HBM, SMEM, HBM, VMEM, HBM, VMEM, VMEM],
        out_specs=VMEM,
        scratch_shapes=[
            pltpu.VMEM((rows + 6, cols, chans), bf16),
            pltpu.VMEM((rows + 2 * SIDE, cols, chans), bf16),
            pltpu.VMEM((rows + 2 * SIDE, cols, chans), bf16),
            pltpu.VMEM((2, rows + 6, cols, cols), bf16),
            pltpu.VMEM((rows + 4, cols, hid), bf16),
            pltpu.VMEM((rows + 2, cols, hid), bf16),
            pltpu.VMEM(w_first.shape, bf16),
            pltpu.VMEM(w_second.shape, bf16),
            pltpu.VMEM((6 * cols, 3 * hid), bf16),
            pltpu.VMEM((3 * hid, 3 * hid), bf16),
            pltpu.VMEM((24, hid), jnp.float32),
            pltpu.SemaphoreType.DMA((copies,)),
            pltpu.SemaphoreType.DMA((copies,)),
            pltpu.SemaphoreType.DMA((3,)),
        ],
        compiler_params=pltpu.CompilerParams(collective_id=0, has_side_effects=True, vmem_limit_bytes=56 << 20),
    )(
        features, offsets, w_first, b_first.reshape(1, hid), w_second, b_second.reshape(1, hid),
        jnp.transpose(w_third, (0, 1, 3, 2)),
    )
    return state + delta[:, None]


def solution(mesh):
    secs, strips = mesh.shape["sec"], mesh.shape["strip"]
    in_specs = (
        P("sec", "strip", None, None),
        P(),
        P(None, "sec", "strip", None),
        P(),
        P(),
        P(),
        P(),
        P(),
    )
    out_specs = P(None, "sec", "strip", None)
    return jax.shard_map(functools.partial(body, secs, strips), mesh=mesh, in_specs=in_specs, out_specs=out_specs, check_vma=False)
```

```python
import functools

import jax
import jax.numpy as jnp
from jax import lax
from jax.experimental import pallas as pl
from jax.experimental.pallas import tpu as pltpu
from jax.sharding import PartitionSpec as P

SIDE = 9
STEP = 3
PIECE = STEP
TAPS = 9
VMEM = pl.BlockSpec(memory_space=pltpu.VMEM)
HBM = pl.BlockSpec(memory_space=pltpu.HBM)
SMEM = pl.BlockSpec(memory_space=pltpu.SMEM)


def group_of(rows):
    return max(g for g in range(1, 8) if rows % g == 0)


def exchange(secs, strips, feat, mine, near, far, send_sem, recv_sem, loads, prepare, turn, relate):
    rows = feat.shape[1]
    count = rows // PIECE
    sec, strip = lax.axis_index("sec"), lax.axis_index("strip")
    odd = lax.rem(sec, 2)
    partner = sec + 1 - 2 * odd
    relay_to, relay_from = sec + 2 - 4 * odd, sec - 2 + 4 * odd
    has_to = (relay_to >= 0) & (relay_to < secs)
    has_from = (relay_from >= 0) & (relay_from < secs)
    has_low, has_high = strip > 0, strip < strips - 1

    barrier = pltpu.get_barrier_semaphore()
    greeted = (
        (None, partner, strip),
        (has_to, relay_to, strip),
        (has_from, relay_from, strip),
        (has_low, sec, strip - 1),
        (has_high, sec, strip + 1),
    )

    def when(cond, act):
        if cond is None:
            act()
        else:
            pl.when(cond)(act)

    for cond, a, b in greeted:
        when(cond, lambda a=a, b=b: pl.semaphore_signal(barrier, inc=1, device_id=(a, b), device_id_type=pl.DeviceIdType.MESH))

    for load in loads:
        load.start()
    pl.semaphore_wait(barrier, 1 + sum(cond.astype(jnp.int32) for cond, _, _ in greeted[1:]))

    waits = []
    number = [0]

    def copy(src, dst, a, b, sends, gets):
        at = number[0]
        number[0] += 1
        made = pltpu.make_async_remote_copy(
            src_ref=src, dst_ref=dst, send_sem=send_sem.at[at], recv_sem=recv_sem.at[at],
            device_id=(a, b), device_id_type=pl.DeviceIdType.MESH,
        )
        when(sends, made.start)
        waits.append((sends, made.wait_send))
        return lambda: when(gets, made.wait_recv)

    def both(x, y):
        return y if x is None else x & y

    def down(slot, q, known):
        return copy(
            slot.at[pl.ds(SIDE + PIECE * q, PIECE)], slot.at[pl.ds(SIDE + rows + PIECE * q, PIECE)],
            sec, strip - 1, both(known, has_low), both(known, has_high),
        )

    def up(slot, q, known):
        return copy(
            slot.at[pl.ds(SIDE + PIECE * q, PIECE)], slot.at[pl.ds(SIDE + PIECE * q - rows, PIECE)],
            sec, strip + 1, both(known, has_high), both(known, has_low),
        )

    order = list(range(count))
    direct = [
        copy(feat.at[0, pl.ds(PIECE * q, PIECE)], near.at[pl.ds(SIDE + PIECE * q, PIECE)], partner, strip, None, None)
        for q in order
    ]
    last = []
    last.append(copy(feat.at[0, pl.ds(0, STEP)], mine.at[pl.ds(STEP + rows, STEP)], sec, strip - 1, has_low, has_high))
    last.append(copy(feat.at[0, pl.ds(rows - STEP, STEP)], mine.at[pl.ds(0, STEP)], sec, strip + 1, has_high, has_low))

    zero = jnp.zeros((SIDE,) + near.shape[1:], near.dtype)

    @pl.when(jnp.logical_not(has_from))
    def _():
        far[...] = jnp.zeros(far.shape, far.dtype)

    @pl.when(jnp.logical_not(has_low))
    def _():
        near[0:SIDE] = zero
        far[0:SIDE] = zero
        mine[0:STEP] = zero[:STEP]

    @pl.when(jnp.logical_not(has_high))
    def _():
        near[SIDE + rows:] = zero
        far[SIDE + rows:] = zero
        mine[STEP + rows:] = zero[:STEP]

    relayed = []
    ends = ([], [])

    def sides(slot, q, known, found):
        if PIECE * q < SIDE:
            found.append(down(slot, q, known))
        if PIECE * q >= rows - SIDE:
            found.append(up(slot, q, known))

    for q in order + [count]:
        if q < count:
            direct[q]()
            relayed.append(copy(
                near.at[pl.ds(SIDE + PIECE * q, PIECE)], far.at[pl.ds(SIDE + PIECE * q, PIECE)],
                relay_to, strip, has_to, has_from,
            ))
            sides(near, q, None, ends[0])
        if q >= 1:
            relayed[q - 1]()
            sides(far, q - 1, has_from, ends[1])
        if q == count // 4:
            prepare()
        if q == count // 2:
            for wait in last:
                wait()
            turn()
    for wide, found, slot in zip((near, far), ends, (1 - odd, odd)):
        for wait in found:
            wait()
        relate(wide, slot)
    for cond, wait in waits:
        when(cond, wait)


def convolve(sources, weight, bias, target):
    rows, cols, width = target.shape
    depth = sources[0].shape[2]
    group = group_of(rows)
    at_col = lax.broadcasted_iota(jnp.int32, (cols, width), 0)

    def step(g, carry):
        base = g * group
        taken = jnp.concatenate(
            [s[pl.ds(base + d, group)].reshape(group * cols, depth) for d in range(3) for s in sources], axis=1
        )
        sums = jnp.dot(taken, weight[...], preferred_element_type=jnp.float32)
        for i in range(group):
            one = sums[i * cols:(i + 1) * cols]
            before = jnp.where(at_col == 0, 0.0, pltpu.roll(one[:, :width], 1, 0))
            after = jnp.where(at_col == cols - 1, 0.0, pltpu.roll(one[:, 2 * width:], cols - 1, 0))
            total = one[:, width:2 * width] + before + after + bias[...]
            target[base + i] = jnp.maximum(total, 0.0).astype(target.dtype)
        return carry

    lax.fori_loop(0, rows // group, step, 0)


def skewed(block, shift):
    rows, cols = block.shape
    pieces = []
    start = 0
    for top in range(0, rows, 8):
        if (shift + top) % cols + 7 > cols:
            if top > start:
                pieces.append(pltpu.roll(block[start:top], (shift + start) % cols, 1, stride=1, stride_axis=0))
            crossing = pltpu.roll(block[top:top + 8], (shift + top - 8) % cols, 1, stride=1, stride_axis=0)
            pieces.append(pltpu.roll(crossing, 8, 1))
            start = top + 8
    if start < rows:
        pieces.append(pltpu.roll(block[start:], (shift + start) % cols, 1, stride=1, stride_axis=0))
    return jnp.concatenate(pieces, axis=0)


def kernel(secs, strips, feat, offsets, w_one, b_one, w_two, b_two, w_three, out,
           mine, near, far, corr, hid_one, hid_two, held_one, held_two, wide_one, wide_two, thirds,
           send_sem, recv_sem, local_sem):
    rows, cols, chans = feat.shape[1:]
    hid = b_one.shape[1]
    planes = w_one.shape[2] // 2
    sec, strip = lax.axis_index("sec"), lax.axis_index("strip")
    loads = [
        pltpu.make_async_copy(feat.at[0], mine.at[pl.ds(STEP, rows)], local_sem.at[0]),
        pltpu.make_async_copy(w_one, held_one, local_sem.at[1]),
        pltpu.make_async_copy(w_two, held_two, local_sem.at[2]),
    ]

    def prepare():
        for d in range(3):
            thirds[8 * d:8 * d + 8] = jnp.zeros((8, hid), thirds.dtype)
            for e in range(3):
                thirds[8 * d + 4 - 2 * e:8 * d + 6 - 2 * e] = w_three[d, e].astype(thirds.dtype)
        for d in range(2 * 3):
            wide_one[d * cols + planes // 16 * 16:(d + 1) * cols] = jnp.zeros((cols - planes // 16 * 16, 3 * hid), wide_one.dtype)
        loads[1].wait()
        loads[2].wait()
        for d in range(3):
            for e in range(3):
                at = pl.ds((2 - e) * hid, hid)
                for j in range(2):
                    wide_one[pl.ds((2 * d + j) * cols, planes), at] = held_one[d, e, j * planes:(j + 1) * planes]
                wide_two[pl.ds(d * hid, hid), at] = held_two[d, e]
        loads[0].wait()

    scale = chans ** (-0.5)
    lane = lax.broadcasted_iota(jnp.int32, (cols, cols), 1)
    col = lax.broadcasted_iota(jnp.int32, (cols, cols), 0)
    flip = (lane + col == cols - 1).astype(mine.dtype)
    other = cols - 1 - col + lax.rem(lane, TAPS) - 4
    gain = jnp.where((other >= 0) & (other < cols) & (lane < planes), scale, 0.0)
    shifts = (
        jnp.where(sec > 0, -offsets[jnp.maximum(sec - 1, 0)], 0),
        jnp.where(sec < secs - 1, offsets[sec], 0),
    )

    def turn():
        def one(r, carry):
            mine[r] = jnp.dot(flip, mine[r], preferred_element_type=jnp.float32).astype(mine.dtype)
            return carry

        lax.fori_loop(0, rows + 6, one, 0)

    group = 6 if rows % 6 == 0 else 2

    def relate(wide, slot):
        shift = jnp.where(slot == 0, shifts[0], shifts[1])

        def step(g, carry):
            base = g * group
            here = mine[pl.ds(base, group)].reshape(group * cols, chans)
            products = {}
            for t in range(0, group + TAPS - 1, 2):
                low, high = max(0, t - TAPS + 1), min(group, t + 2)
                there = wide[pl.ds(base + 2 + shift + t, 2)].reshape(2 * cols, chans)
                tile = lax.dot_general(
                    here[low * cols:high * cols], there, (((1,), (1,)), ((), ())), preferred_element_type=jnp.float32
                )
                for i in range(low, high):
                    for u in range(2):
                        if 0 <= t + u - i < TAPS:
                            products[i, t + u - i] = tile[(i - low) * cols:(i - low + 1) * cols, u * cols:(u + 1) * cols]
            for i in range(group):
                found = skewed(products[i, 0], 5)
                for a in range(1, TAPS):
                    found = jnp.where(lane >= a * TAPS, skewed(products[i, a], a * TAPS + 5), found)
                corr[slot, base + i] = (found * gain).astype(corr.dtype)
            return carry

        lax.fori_loop(0, (rows + 6) // group, step, 0)

    exchange(secs, strips, feat, mine, near, far, send_sem, recv_sem, loads, prepare, turn, relate)

    convolve((corr.at[0], corr.at[1]), wide_one, b_one, hid_one)

    @pl.when(strip == 0)
    def _():
        hid_one[0:2] = jnp.zeros((2, cols, hid), hid_one.dtype)

    @pl.when(strip == strips - 1)
    def _():
        hid_one[rows + 2:] = jnp.zeros((2, cols, hid), hid_one.dtype)

    convolve((hid_one,), wide_two, b_two, hid_two)

    @pl.when(strip == 0)
    def _():
        hid_two[0:1] = jnp.zeros((1, cols, hid), hid_two.dtype)

    @pl.when(strip == strips - 1)
    def _():
        hid_two[rows + 1:] = jnp.zeros((1, cols, hid), hid_two.dtype)

    taps = lax.dot_general(
        thirds[...].astype(hid_two.dtype), hid_two[...].reshape((rows + 2) * cols, hid), (((1,), (1,)), ((), ())),
        preferred_element_type=jnp.float32,
    )
    at_lane = lax.broadcasted_iota(jnp.int32, (8, cols), 1)
    found = []
    for r in range(rows):
        total = sum(taps[8 * d:8 * d + 8, (r + d) * cols:(r + d + 1) * cols] for d in range(3))
        before = jnp.where(at_lane == 0, 0.0, pltpu.roll(total, 1, 1))
        after = jnp.where(at_lane == cols - 1, 0.0, pltpu.roll(total, cols - 1, 1))
        found.append(before[0:2] + total[2:4] + after[4:6])
    turned = jnp.dot(
        jnp.concatenate(found, axis=0), flip.astype(jnp.float32),
        preferred_element_type=jnp.float32, precision=lax.Precision.HIGHEST,
    )
    for r in range(rows):
        for p in range(2):
            out[p * rows + r] = turned[2 * r + p:2 * r + p + 1]


def body(secs, strips, features, offsets, state, w_first, b_first, w_second, b_second, w_third):
    _, rows, cols, chans = features.shape
    hid = w_first.shape[3]
    parts = w_third.shape[3]
    copies = 2 * (rows // PIECE) + 4 * (SIDE // PIECE) + 2
    bf16 = jnp.bfloat16
    delta = pl.pallas_call(
        functools.partial(kernel, secs, strips),
        out_shape=jax.ShapeDtypeStruct((parts * rows, 1, cols), jnp.float32),
        in_specs=[HBM, SMEM, HBM, VMEM, HBM, VMEM, VMEM],
        out_specs=VMEM,
        scratch_shapes=[
            pltpu.VMEM((rows + 6, cols, chans), bf16),
            pltpu.VMEM((rows + 2 * SIDE, cols, chans), bf16),
            pltpu.VMEM((rows + 2 * SIDE, cols, chans), bf16),
            pltpu.VMEM((2, rows + 6, cols, cols), bf16),
            pltpu.VMEM((rows + 4, cols, hid), bf16),
            pltpu.VMEM((rows + 2, cols, hid), bf16),
            pltpu.VMEM(w_first.shape, bf16),
            pltpu.VMEM(w_second.shape, bf16),
            pltpu.VMEM((6 * cols, 3 * hid), bf16),
            pltpu.VMEM((3 * hid, 3 * hid), bf16),
            pltpu.VMEM((24, hid), jnp.float32),
            pltpu.SemaphoreType.DMA((copies,)),
            pltpu.SemaphoreType.DMA((copies,)),
            pltpu.SemaphoreType.DMA((3,)),
        ],
        compiler_params=pltpu.CompilerParams(collective_id=0, has_side_effects=True, vmem_limit_bytes=56 << 20),
    )(
        features, offsets, w_first, b_first.reshape(1, hid), w_second, b_second.reshape(1, hid),
        jnp.transpose(w_third, (0, 1, 3, 2)),
    )
    return state + delta.reshape(state.shape)


def solution(mesh):
    secs, strips = mesh.shape["sec"], mesh.shape["strip"]
    in_specs = (
        P("sec", "strip", None, None),
        P(),
        P(None, "sec", "strip", None),
        P(),
        P(),
        P(),
        P(),
        P(),
    )
    out_specs = P(None, "sec", "strip", None)
    return jax.shard_map(functools.partial(body, secs, strips), mesh=mesh, in_specs=in_specs, out_specs=out_specs, check_vma=False)
```

```python
import functools

import jax
import jax.numpy as jnp
from jax import lax
from jax.experimental import pallas as pl
from jax.experimental.pallas import tpu as pltpu
from jax.sharding import PartitionSpec as P

SIDE = 9
STEP = 3
PIECE = STEP
TAPS = 9
VMEM = pl.BlockSpec(memory_space=pltpu.VMEM)
HBM = pl.BlockSpec(memory_space=pltpu.HBM)
SMEM = pl.BlockSpec(memory_space=pltpu.SMEM)


def group_of(rows):
    return max(g for g in range(1, 8) if rows % g == 0)


def exchange(secs, strips, feat, mine, near, far, send_sem, recv_sem, loads, prepare, turn, own, relate):
    rows = feat.shape[1]
    count = rows // PIECE
    sec, strip = lax.axis_index("sec"), lax.axis_index("strip")
    odd = lax.rem(sec, 2)
    partner = sec + 1 - 2 * odd
    relay_to, relay_from = sec + 2 - 4 * odd, sec - 2 + 4 * odd
    has_to = (relay_to >= 0) & (relay_to < secs)
    has_from = (relay_from >= 0) & (relay_from < secs)
    has_low, has_high = strip > 0, strip < strips - 1

    barrier = pltpu.get_barrier_semaphore()
    greeted = (
        (None, partner, strip),
        (has_to, relay_to, strip),
        (has_from, relay_from, strip),
        (has_low, sec, strip - 1),
        (has_high, sec, strip + 1),
    )

    def when(cond, act):
        if cond is None:
            act()
        else:
            pl.when(cond)(act)

    for cond, a, b in greeted:
        when(cond, lambda a=a, b=b: pl.semaphore_signal(barrier, inc=1, device_id=(a, b), device_id_type=pl.DeviceIdType.MESH))

    for load in loads:
        load.start()
    pl.semaphore_wait(barrier, 1 + sum(cond.astype(jnp.int32) for cond, _, _ in greeted[1:]))

    waits = []
    number = [0]

    def copy(src, dst, a, b, sends, gets):
        at = number[0]
        number[0] += 1
        made = pltpu.make_async_remote_copy(
            src_ref=src, dst_ref=dst, send_sem=send_sem.at[at], recv_sem=recv_sem.at[at],
            device_id=(a, b), device_id_type=pl.DeviceIdType.MESH,
        )
        when(sends, made.start)
        waits.append((sends, made.wait_send))
        return lambda: when(gets, made.wait_recv)

    def both(x, y):
        return y if x is None else x & y

    def down(slot, q, known):
        return copy(
            slot.at[pl.ds(SIDE + PIECE * q, PIECE)], slot.at[pl.ds(SIDE + rows + PIECE * q, PIECE)],
            sec, strip - 1, both(known, has_low), both(known, has_high),
        )

    def up(slot, q, known):
        return copy(
            slot.at[pl.ds(SIDE + PIECE * q, PIECE)], slot.at[pl.ds(SIDE + PIECE * q - rows, PIECE)],
            sec, strip + 1, both(known, has_high), both(known, has_low),
        )

    order = list(range(count))
    direct = [
        copy(feat.at[0, pl.ds(PIECE * q, PIECE)], near.at[pl.ds(SIDE + PIECE * q, PIECE)], partner, strip, None, None)
        for q in order
    ]
    last = []
    last.append(copy(feat.at[0, pl.ds(0, STEP)], mine.at[pl.ds(STEP + rows, STEP)], sec, strip - 1, has_low, has_high))
    last.append(copy(feat.at[0, pl.ds(rows - STEP, STEP)], mine.at[pl.ds(0, STEP)], sec, strip + 1, has_high, has_low))

    zero = jnp.zeros((SIDE,) + near.shape[1:], near.dtype)

    @pl.when(jnp.logical_not(has_from))
    def _():
        far[...] = jnp.zeros(far.shape, far.dtype)

    @pl.when(jnp.logical_not(has_low))
    def _():
        near[0:SIDE] = zero
        far[0:SIDE] = zero
        mine[0:STEP] = zero[:STEP]

    @pl.when(jnp.logical_not(has_high))
    def _():
        near[SIDE + rows:] = zero
        far[SIDE + rows:] = zero
        mine[STEP + rows:] = zero[:STEP]

    relayed = []
    ends = ([], [])

    def sides(slot, q, known, found):
        if PIECE * q < SIDE:
            found.append(down(slot, q, known))
        if PIECE * q >= rows - SIDE:
            found.append(up(slot, q, known))

    for q in order + [count]:
        if q < count:
            direct[q]()
            relayed.append(copy(
                near.at[pl.ds(SIDE + PIECE * q, PIECE)], far.at[pl.ds(SIDE + PIECE * q, PIECE)],
                relay_to, strip, has_to, has_from,
            ))
            sides(near, q, None, ends[0])
        if q >= 1:
            relayed[q - 1]()
            sides(far, q - 1, has_from, ends[1])
        if q == count // 4:
            prepare()
        if q == count // 2:
            for wait in last:
                wait()
            turn()
            own(near, 1 - odd, 0, rows // 4)
    own(near, 1 - odd, rows // 4, rows // 2)
    for wide, found, slot in zip((near, far), ends, (1 - odd, odd)):
        for wait in found:
            wait()
        if wide is far:
            own(far, odd, 0, rows // 2)
        relate(wide, slot)
    for cond, wait in waits:
        when(cond, wait)


def convolve(sources, weight, bias, target):
    rows, cols, width = target.shape
    depth = sources[0].shape[2]
    group = group_of(rows)
    at_col = lax.broadcasted_iota(jnp.int32, (cols, width), 0)

    def step(g, carry):
        base = g * group
        taken = jnp.concatenate(
            [s[pl.ds(base + d, group)].reshape(group * cols, depth) for d in range(3) for s in sources], axis=1
        )
        sums = jnp.dot(taken, weight[...], preferred_element_type=jnp.float32)
        for i in range(group):
            one = sums[i * cols:(i + 1) * cols]
            before = jnp.where(at_col == 0, 0.0, pltpu.roll(one[:, :width], 1, 0))
            after = jnp.where(at_col == cols - 1, 0.0, pltpu.roll(one[:, 2 * width:], cols - 1, 0))
            total = one[:, width:2 * width] + before + after + bias[...]
            target[base + i] = jnp.maximum(total, 0.0).astype(target.dtype)
        return carry

    lax.fori_loop(0, rows // group, step, 0)


def skewed(block, shift):
    rows, cols = block.shape
    pieces = []
    start = 0
    for top in range(0, rows, 8):
        if (shift + top) % cols + 7 > cols:
            if top > start:
                pieces.append(pltpu.roll(block[start:top], (shift + start) % cols, 1, stride=1, stride_axis=0))
            crossing = pltpu.roll(block[top:top + 8], (shift + top - 8) % cols, 1, stride=1, stride_axis=0)
            pieces.append(pltpu.roll(crossing, 8, 1))
            start = top + 8
    if start < rows:
        pieces.append(pltpu.roll(block[start:], (shift + start) % cols, 1, stride=1, stride_axis=0))
    return jnp.concatenate(pieces, axis=0)


def kernel(secs, strips, feat, offsets, w_one, b_one, w_two, b_two, w_three, out,
           mine, turned, total, near, far, corr, hid_one, hid_two, held_one, held_two, wide_one, wide_two, thirds,
           send_sem, recv_sem, local_sem):
    rows, cols, chans = feat.shape[1:]
    hid = b_one.shape[1]
    planes = w_one.shape[2] // 2
    sec, strip = lax.axis_index("sec"), lax.axis_index("strip")
    loads = [
        pltpu.make_async_copy(feat.at[0], mine.at[pl.ds(STEP, rows)], local_sem.at[0]),
        pltpu.make_async_copy(w_one, held_one, local_sem.at[1]),
        pltpu.make_async_copy(w_two, held_two, local_sem.at[2]),
    ]

    def prepare():
        for d in range(3):
            thirds[8 * d:8 * d + 8] = jnp.zeros((8, hid), thirds.dtype)
            for e in range(3):
                thirds[8 * d + 4 - 2 * e:8 * d + 6 - 2 * e] = w_three[d, e].astype(thirds.dtype)
        for d in range(2 * 3):
            wide_one[d * cols + planes // 16 * 16:(d + 1) * cols] = jnp.zeros((cols - planes // 16 * 16, 3 * hid), wide_one.dtype)
        loads[1].wait()
        loads[2].wait()
        for d in range(3):
            for e in range(3):
                at = pl.ds((2 - e) * hid, hid)
                for j in range(2):
                    wide_one[pl.ds((2 * d + j) * cols, planes), at] = held_one[d, e, j * planes:(j + 1) * planes]
                wide_two[pl.ds(d * hid, hid), at] = held_two[d, e]
        loads[0].wait()

    scale = chans ** (-0.5)
    lane = lax.broadcasted_iota(jnp.int32, (cols, cols), 1)
    col = lax.broadcasted_iota(jnp.int32, (cols, cols), 0)
    flip = (lane + col == cols - 1).astype(mine.dtype)
    other = cols - 1 - col + lax.rem(lane, TAPS) - 4
    gain = jnp.where((other >= 0) & (other < cols) & (lane < planes), scale, 0.0)
    shifts = (
        jnp.where(sec > 0, -offsets[jnp.maximum(sec - 1, 0)], 0),
        jnp.where(sec < secs - 1, offsets[sec], 0),
    )

    spans = rows + 10

    def turn():
        turned[0:4] = jnp.zeros((4, cols, chans), turned.dtype)
        turned[rows + 10:] = jnp.zeros((4, cols, chans), turned.dtype)

        def one(r, carry):
            turned[r + 4] = jnp.dot(flip, mine[r], preferred_element_type=jnp.float32).astype(mine.dtype)
            return carry

        lax.fori_loop(0, rows + 6, one, 0)

        def clear(r, carry):
            for slot in range(2):
                total[slot, r] = jnp.zeros((cols, cols), jnp.float32)
            return carry

        lax.fori_loop(0, spans, clear, 0)

    def shift_of(slot):
        return jnp.where(slot == 0, shifts[0], shifts[1])

    def block(wide, slot, at, wides, start, number):
        here = turned[pl.ds(start + 2 - shift_of(slot), number)].reshape(number * cols, chans)
        there = wide[pl.ds(at, wides)].reshape(wides * cols, chans)
        tile = lax.dot_general(here, there, (((1,), (1,)), ((), ())), preferred_element_type=jnp.float32)
        for i in range(number):
            found = total[slot, start + i]
            for u in range(wides):
                a = at + u - start - i
                if 0 <= a < TAPS:
                    band = skewed(tile[i * cols:(i + 1) * cols, u * cols:(u + 1) * cols], a * TAPS + 5)
                    found = jnp.where((lane >= a * TAPS) & (lane < a * TAPS + TAPS), band, found)
            total[slot, start + i] = found

    def own(wide, slot, begin, end):
        def step(k, carry):
            at = SIDE + 2 * k
            here = turned[pl.ds(at - 6 - shift_of(slot), 10)].reshape(10 * cols, chans)
            there = wide[pl.ds(at, 2)].reshape(2 * cols, chans)
            tile = lax.dot_general(here, there, (((1,), (1,)), ((), ())), preferred_element_type=jnp.float32)
            for i in range(10):
                found = total[slot, at - 8 + i]
                for u in range(2):
                    a = 8 + u - i
                    if 0 <= a < TAPS:
                        band = skewed(tile[i * cols:(i + 1) * cols, u * cols:(u + 1) * cols], a * TAPS + 5)
                        found = jnp.where((lane >= a * TAPS) & (lane < a * TAPS + TAPS), band, found)
                total[slot, at - 8 + i] = found
            return carry

        lax.fori_loop(begin, end, step, 0)

    def relate(wide, slot):
        block(wide, slot, 0, 1, 0, 1)
        for at in range(1, SIDE, 2):
            start = max(0, at - 8)
            block(wide, slot, at, 2, start, at + 2 - start)
        for at in range(SIDE + rows, 2 * SIDE + rows - 1, 2):
            block(wide, slot, at, 2, at - 8, min(spans, at + 2) - at + 8)
        at = 2 * SIDE + rows - 1
        block(wide, slot, at, 1, at - 8, spans - at + 8)

        def finish(r, carry):
            corr[slot, r] = jnp.where(gain > 0, total[slot, r + 2 + shift_of(slot)] * scale, 0.0).astype(corr.dtype)
            return carry

        lax.fori_loop(0, rows + 6, finish, 0)

    exchange(secs, strips, feat, mine, near, far, send_sem, recv_sem, loads, prepare, turn, own, relate)

    convolve((corr.at[0], corr.at[1]), wide_one, b_one, hid_one)

    @pl.when(strip == 0)
    def _():
        hid_one[0:2] = jnp.zeros((2, cols, hid), hid_one.dtype)

    @pl.when(strip == strips - 1)
    def _():
        hid_one[rows + 2:] = jnp.zeros((2, cols, hid), hid_one.dtype)

    convolve((hid_one,), wide_two, b_two, hid_two)

    @pl.when(strip == 0)
    def _():
        hid_two[0:1] = jnp.zeros((1, cols, hid), hid_two.dtype)

    @pl.when(strip == strips - 1)
    def _():
        hid_two[rows + 1:] = jnp.zeros((1, cols, hid), hid_two.dtype)

    taps = lax.dot_general(
        thirds[...].astype(hid_two.dtype), hid_two[...].reshape((rows + 2) * cols, hid), (((1,), (1,)), ((), ())),
        preferred_element_type=jnp.float32,
    )
    at_lane = lax.broadcasted_iota(jnp.int32, (8, cols), 1)
    found = []
    for r in range(rows):
        total = sum(taps[8 * d:8 * d + 8, (r + d) * cols:(r + d + 1) * cols] for d in range(3))
        before = jnp.where(at_lane == 0, 0.0, pltpu.roll(total, 1, 1))
        after = jnp.where(at_lane == cols - 1, 0.0, pltpu.roll(total, cols - 1, 1))
        found.append(before[0:2] + total[2:4] + after[4:6])
    straight = jnp.dot(
        jnp.concatenate(found, axis=0), flip.astype(jnp.float32),
        preferred_element_type=jnp.float32, precision=lax.Precision.HIGHEST,
    )
    for r in range(rows):
        for p in range(2):
            out[p * rows + r] = straight[2 * r + p:2 * r + p + 1]


def body(secs, strips, features, offsets, state, w_first, b_first, w_second, b_second, w_third):
    _, rows, cols, chans = features.shape
    hid = w_first.shape[3]
    parts = w_third.shape[3]
    copies = 2 * (rows // PIECE) + 4 * (SIDE // PIECE) + 2
    bf16 = jnp.bfloat16
    delta = pl.pallas_call(
        functools.partial(kernel, secs, strips),
        out_shape=jax.ShapeDtypeStruct((parts * rows, 1, cols), jnp.float32),
        in_specs=[HBM, SMEM, HBM, VMEM, HBM, VMEM, VMEM],
        out_specs=VMEM,
        scratch_shapes=[
            pltpu.VMEM((rows + 6, cols, chans), bf16),
            pltpu.VMEM((rows + 14, cols, chans), bf16),
            pltpu.VMEM((2, rows + 10, cols, cols), jnp.float32),
            pltpu.VMEM((rows + 2 * SIDE, cols, chans), bf16),
            pltpu.VMEM((rows + 2 * SIDE, cols, chans), bf16),
            pltpu.VMEM((2, rows + 6, cols, cols), bf16),
            pltpu.VMEM((rows + 4, cols, hid), bf16),
            pltpu.VMEM((rows + 2, cols, hid), bf16),
            pltpu.VMEM(w_first.shape, bf16),
            pltpu.VMEM(w_second.shape, bf16),
            pltpu.VMEM((6 * cols, 3 * hid), bf16),
            pltpu.VMEM((3 * hid, 3 * hid), bf16),
            pltpu.VMEM((24, hid), jnp.float32),
            pltpu.SemaphoreType.DMA((copies,)),
            pltpu.SemaphoreType.DMA((copies,)),
            pltpu.SemaphoreType.DMA((3,)),
        ],
        compiler_params=pltpu.CompilerParams(collective_id=0, has_side_effects=True, vmem_limit_bytes=56 << 20),
    )(
        features, offsets, w_first, b_first.reshape(1, hid), w_second, b_second.reshape(1, hid),
        jnp.transpose(w_third, (0, 1, 3, 2)),
    )
    return state + delta.reshape(state.shape)


def solution(mesh):
    secs, strips = mesh.shape["sec"], mesh.shape["strip"]
    in_specs = (
        P("sec", "strip", None, None),
        P(),
        P(None, "sec", "strip", None),
        P(),
        P(),
        P(),
        P(),
        P(),
    )
    out_specs = P(None, "sec", "strip", None)
    return jax.shard_map(functools.partial(body, secs, strips), mesh=mesh, in_specs=in_specs, out_specs=out_specs, check_vma=False)
```
